32 devices in a mesh: groups: 2 (over x), blk: 16 (over z, y, core).
Axes of the slice: x: 2, y: 2, z: 4, core: 2. Of those that a mesh axis runs over, the one named last changes fastest.
Arguments:
- queries: bfloat16 [24576, 1536], P(('groups', 'blk')), parts along dimension 0, may hold values from -20 to 20
- keys: bfloat16 [24576, 1536], P(('groups', 'blk')), parts along dimension 0, may hold values from -6 to 6
- values: bfloat16 [24576, 1536], P(('groups', 'blk')), parts along dimension 0, may hold values from -6 to 6
- neighbours: int32 [64, 7], P(('groups', 'blk')), parts along dimension 0, may hold values from -1 to 31, as said below
Outputs:
- attended: bfloat16 [24576, 1536], P(('groups', 'blk')), parts along dimension 0
The draws below stay inside these ranges and needn't reach their ends.
There are 2 independent parts, one for each index of `groups`. The reference program is written for one: setup_inputs(seed, part) draws one part's arguments, and reference() takes and returns one part's arrays. A program takes and returns all parts, laid end to end along the dimension named above; each array names one. Nothing has to cross between parts.
Inputs may be any that keep to these rules, and one draw needn't show every extreme that they name: `neighbours`: entry 0 of row t is t itself. Every other non-negative entry names a distinct tile of a frame block at most two blocks away from tile t's block; a slot is -1 only where its drawn tile falls outside the clip.
All inputs are finite; a program needn't handle non-finite values.
Results may differ from the reference program's by a relative error of at most 0.0048.
Values may be sent and summed in bfloat16 or wider, within the bound.
A program may use at most 128 MiB of HBM per device.

```python
import jax
import jax.numpy as jnp
from jax import lax

HEADS = 12
HD = 128
TILE = 384
NBR = 7
TILES_DEV = 2
TILES = 32
TOKENS = 12288


def query_key_pair(key):
    query_key = jax.random.fold_in(key, 11)
    key_key = jax.random.fold_in(key, 12)
    shape = (TOKENS, HEADS * HD)
    keys_drawn = jnp.clip(jax.random.normal(key_key, shape, jnp.float32), -6.0, 6.0)
    queries_drawn = jnp.clip(jax.random.normal(query_key, shape, jnp.float32), -6.0, 6.0)
    return (queries_drawn, keys_drawn)


def draw_queries(key, part):
    return query_key_pair(key)[0].astype(jnp.bfloat16)


def draw_keys(key, part):
    return query_key_pair(key)[1].astype(jnp.bfloat16)


def draw_neighbours(key, part):
    candidates = 5 * TILES_DEV
    rows = jnp.arange(TILES, dtype=jnp.int32)
    block = rows // TILES_DEV
    base = (block - 2) * TILES_DEV
    own_offset = rows - base
    row_keys = jax.random.split(jax.random.fold_in(key, 21), TILES)
    picks = jax.vmap(lambda row_key: jax.random.permutation(row_key, candidates - 1))(row_keys)[:, :NBR - 1]
    offsets = picks + (picks >= own_offset[:, None]).astype(jnp.int32)
    others = base[:, None] + offsets
    others = jnp.where((others >= 0) & (others < TILES), others, -1)
    return jnp.concatenate([rows[:, None], others], axis=1).astype(jnp.int32)


def level_of(own_key, extent, cuts, low, largest):
    def one(dim, parts):
        steps = jax.random.uniform(jax.random.fold_in(jax.random.fold_in(own_key, 6), dim), (parts,), jnp.float32, low / len(cuts), largest / len(cuts))
        return jnp.repeat(jnp.exp(steps), extent[dim] // parts).reshape((-1,) + (1,) * (len(extent) - dim - 1))

    loudness = one(*cuts[0])
    for cut in cuts[1:]:
        loudness = loudness * one(*cut)
    return loudness


def scatter_about(stream_key, extent, deviation, most, cuts=(), kind=jnp.bfloat16):
    loudness = level_of(stream_key, extent, cuts, -0.22, 0.18) if cuts else 1.0
    array = jax.random.normal(stream_key, extent, jnp.float32) * deviation * loudness
    return jnp.minimum(jnp.maximum(array, -most), most).astype(kind)


def setup_inputs(seed: int = 0, part: int = 0) -> dict:
    arg_keys = jax.random.split(jax.random.key(seed), 5)
    part_splits = jax.random.split(jax.random.fold_in(arg_keys[4], part), 5)
    return {
        "queries": draw_queries(jax.random.fold_in(jax.random.fold_in(arg_keys[4], part), 71), part),
        "keys": draw_keys(jax.random.fold_in(jax.random.fold_in(arg_keys[4], part), 71), part),
        "values": scatter_about(part_splits[2], (TOKENS, HEADS * HD), 1.0, 6.0, ((0, 16),)),
        "neighbours": draw_neighbours(jax.random.fold_in(jax.random.fold_in(arg_keys[4], part), 71), part),
    }


def reference(queries, keys, values, neighbours):
    scale = HD ** -0.5
    q_tiles = queries.reshape(TILES, TILE, HEADS, HD)
    k_tiles = keys.reshape(TILES, TILE, HEADS, HD)
    v_tiles = values.reshape(TILES, TILE, HEADS, HD)

    def one_tile(tile_id):
        named = neighbours[tile_id]
        valid = named >= 0
        safe = jnp.where(valid, named, 0).astype(jnp.int32)
        key_rows = k_tiles[safe].reshape(NBR * TILE, HEADS, HD).astype(jnp.float32)
        value_rows = v_tiles[safe].reshape(NBR * TILE, HEADS, HD).astype(jnp.float32)
        query_rows = q_tiles[tile_id].astype(jnp.float32)
        scores = jnp.einsum("qhd,khd->hqk", query_rows, key_rows) * scale
        key_mask = jnp.repeat(valid, TILE)
        scores = jnp.where(key_mask[None, None, :], scores, -jnp.inf)
        peak = jnp.max(scores, axis=2, keepdims=True)
        weights = jnp.exp(scores - peak)
        total = jnp.sum(weights, axis=2)
        rounded = lax.optimization_barrier(weights.astype(jnp.bfloat16)).astype(jnp.float32)
        summed = jnp.einsum("hqk,khd->qhd", rounded, value_rows)
        result = summed / jnp.transpose(total)[:, :, None]
        return result.astype(jnp.bfloat16).reshape(TILE, HEADS * HD)

    output = lax.map(one_tile, jnp.arange(TILES, dtype=jnp.int32))
    return output.reshape(TILES * TILE, HEADS * HD)
```

```python
import functools
import math

import jax
import jax.numpy as jnp
from jax import lax
from jax.experimental import pallas as pl
from jax.experimental.pallas import tpu as pltpu
from jax.sharding import PartitionSpec as P

HD = 128
WINDOW = 5
PIECES = 4


def kernel(count, heads, named, queries, keys, values, out, *scratch):
    windows = (scratch[:heads], scratch[heads : 2 * heads])
    (scores, tops, held_q, held_o, local_sem, q_sem, o_sem, y_send, y_recv, sib_send, sib_recv,
     z_send, z_recv, share_send, share_recv) = scratch[2 * heads :]
    sources = (keys, values)
    tiles, tile_len, _ = queries.shape
    slots = named.shape[1]
    rows = tile_len // PIECES
    per_tile = PIECES // tiles
    factor = math.log2(math.e) * HD ** -0.5

    me = lax.axis_index("blk")
    core = lax.rem(me, 2)
    side = lax.rem(me // 2, 2)
    quad = me // 4
    last = count // 4 - 1
    sibling = me + 1 - 2 * core
    partner = me + 2 - 4 * side
    ahead = me + 4 - 8 * side
    behind = me - 4 + 8 * side
    can_relay = jnp.where(side == 0, quad < last, quad > 0)
    gets_relay = jnp.where(side == 0, quad > 0, quad < last)
    shares_partner = core == side
    shares_relay = jnp.logical_and(jnp.logical_not(shares_partner), gets_relay)
    partner_at = 4 - 4 * side
    relay_at = 4 * side

    def strip(head):
        return pl.ds(head * HD, HD)

    def part(ref, block, piece=None):
        at = pl.ds(block * tiles, tiles)
        return ref.at[at] if piece is None else ref.at[at, pl.ds(piece * rows, rows)]

    def remote(src, dst, send, recv, target):
        return pltpu.make_async_remote_copy(
            src_ref=src, dst_ref=dst, send_sem=send, recv_sem=recv,
            device_id={"blk": target}, device_id_type=pl.DeviceIdType.MESH,
        )

    def partner_copy(head, which, piece=None):
        window = windows[which][head]
        if piece is None:
            src = sources[which].at[:, :, strip(head)]
        else:
            src = sources[which].at[:, pl.ds(piece * rows, rows), strip(head)]
        recv = y_recv.at[head, which, 0 if piece is None else piece]
        return remote(src, part(window, relay_at, piece), y_send.at[head, which], recv, partner)

    def relay_copy(head, which, piece=None):
        window = windows[which][head]
        recv = z_recv.at[head, which, 0 if piece is None else piece]
        return remote(part(window, partner_at, piece), part(window, relay_at, piece),
                      z_send.at[head, which], recv, ahead)

    def share_copy(head, which, piece=None):
        window = windows[which][head]
        return remote(part(window, 4 - 4 * core, piece), part(window, 3 - 2 * core, piece),
                      share_send.at[head, which], share_recv.at[head, which], sibling)

    def sibling_copy(head, which, tile=None):
        window, source = windows[which][head], sources[which]
        at = (1 + 2 * core) * tiles
        if tile is None:
            src, dst = source.at[:, :, strip(head)], window.at[pl.ds(at, tiles)]
        else:
            src, dst = source.at[tile, :, strip(head)], window.at[at + tile]
        return remote(src, dst, sib_send.at[head, which], sib_recv.at[head, which], sibling)

    def local_copy(head, which, tile=None):
        window, source = windows[which][head], sources[which]
        if tile is None:
            src, dst = source.at[:, :, strip(head)], part(window, 2)
        else:
            src, dst = source.at[tile, :, strip(head)], window.at[2 * tiles + tile]
        return pltpu.make_async_copy(src, dst, local_sem.at[head, which])

    def query_copy(head, tile=None):
        if tile is None:
            return pltpu.make_async_copy(queries.at[:, :, strip(head)], held_q.at[:, :, strip(head)], q_sem.at[head])
        return pltpu.make_async_copy(
            queries.at[tile, :, strip(head)], held_q.at[tile, :, strip(head)], q_sem.at[head])

    def out_copy(head, tile=None):
        if tile is None:
            return pltpu.make_async_copy(held_o.at[:, :, strip(head)], out.at[:, :, strip(head)], o_sem.at[head])
        return pltpu.make_async_copy(
            held_o.at[tile, :, strip(head)], out.at[tile, :, strip(head)], o_sem.at[head])

    def send(head, which, tile):
        for j in range(per_tile):
            partner_copy(head, which, tile * per_tile + j).start()
        sibling_copy(head, which, tile).start()
        local_copy(head, which, tile).start()
        if which == 0:
            query_copy(head, tile).start()

    def pass_on(head, which, piece):
        partner_copy(head, which, piece).wait_recv()

        @pl.when(can_relay)
        def _():
            relay_copy(head, which, piece).start()

        @pl.when(shares_partner)
        def _():
            share_copy(head, which, piece).start()

    def share_relay(head, which, piece):
        @pl.when(shares_relay)
        def _():
            relay_copy(head, which, piece).wait_recv()
            share_copy(head, which, piece).start()

    def gather(head, which):
        local_copy(head, which).wait()
        sibling_copy(head, which).wait_recv()

        @pl.when(jnp.logical_and(shares_partner, gets_relay))
        def _():
            for piece in range(PIECES):
                relay_copy(head, which, piece).wait_recv()

        @pl.when(jnp.logical_or(jnp.logical_not(shares_partner), gets_relay))
        def _():
            share_copy(head, which).wait_recv()

    def drain(head):
        for which in range(2):
            partner_copy(head, which).wait_send()
            sibling_copy(head, which).wait_send()

            @pl.when(can_relay)
            def _():
                relay_copy(head, which).wait_send()

            @pl.when(jnp.logical_or(shares_partner, gets_relay))
            def _():
                share_copy(head, which).wait_send()

    def place_of(tile, slot):
        entry = named[tile, slot]
        ok = entry >= 0
        place = jnp.where(ok, entry - (me - 2) * tiles, 2 * tiles + tile)
        return ok, jnp.clip(place, 0, WINDOW * tiles - 1)

    def score(head, tile):
        query = held_q[tile, :, strip(head)]
        peaks = []
        for slot in range(slots):
            ok, place = place_of(tile, slot)
            score = lax.dot_general(
                query, windows[0][head][place], (((1,), (1,)), ((), ())),
                preferred_element_type=jnp.float32,
            )
            scores[tile, slot] = score
            peaks.append(jnp.where(ok, jnp.max(score, axis=1, keepdims=True), -jnp.inf))
        tops[tile] = jnp.broadcast_to(functools.reduce(jnp.maximum, peaks) * factor, tops.shape[1:])

    def mix(head, tile):
        total = jnp.zeros((tile_len, 1), jnp.float32)
        summed = jnp.zeros((tile_len, HD), jnp.float32)
        top = tops[tile, :, 0:1]
        for slot in range(slots):
            ok, place = place_of(tile, slot)
            offset = jnp.where(ok, top, jnp.inf)
            weights = jnp.exp2(scores[tile, slot] * factor - offset)
            total += jnp.sum(weights, axis=1, keepdims=True)
            summed += jnp.dot(
                weights.astype(jnp.bfloat16), windows[1][head][place],
                preferred_element_type=jnp.float32,
            )
        held_o[tile, :, strip(head)] = (summed / total).astype(held_o.dtype)

    barrier = pltpu.get_barrier_semaphore()

    def greet(target):
        pl.semaphore_signal(barrier, inc=1, device_id={"blk": target}, device_id_type=pl.DeviceIdType.MESH)

    greet(partner)
    greet(sibling)

    @pl.when(gets_relay)
    def _():
        greet(behind)

    pl.semaphore_wait(barrier, 2 + can_relay.astype(jnp.int32))

    for which in range(2):
        for tile in range(tiles):
            send(0, which, tile)

    for step in range(heads + 1):
        head = step - 1
        for which in range(2):
            if step == heads:
                for piece in range(PIECES):
                    if which == 0:
                        share_relay(head, 1, piece)

            @pl.loop(0, tiles)
            def _(tile):
                for j in range(per_tile):
                    piece = tile * per_tile + j
                    if step < heads:
                        pass_on(step, which, piece)
                        if which == 1:
                            share_relay(step, 0, piece)
                        elif head >= 0:
                            share_relay(head, 1, piece)
                    if j == 0:
                        if step + 1 < heads:
                            send(step + 1, which, tile)
                        if head > 0 and which == 0:
                            @pl.when(tile == tiles - 1)
                            def _():
                                drain(head - 1)
                if head >= 0:
                    @pl.when(tile == 0)
                    def _():
                        if which == 0:
                            query_copy(head).wait()
                        gather(head, which)

                    if which == 0:
                        score(head, tile)
                    else:
                        mix(head, tile)
                        out_copy(head, tile).start()

    drain(heads - 1)
    for head in range(heads):
        out_copy(head).wait()


def on_device(count, queries, keys, values, neighbours):
    tokens, width = queries.shape
    tiles, slots = neighbours.shape
    tile_len = tokens // tiles
    heads = width // HD
    shape = (tiles, tile_len, width)
    window = pltpu.VMEM((WINDOW * tiles, tile_len, HD), queries.dtype)
    single = pltpu.SemaphoreType.DMA((heads,))
    pair = pltpu.SemaphoreType.DMA((heads, 2))
    each = pltpu.SemaphoreType.DMA((heads, 2, PIECES))
    hbm = pl.BlockSpec(memory_space=pl.ANY)
    out = pl.pallas_call(
        functools.partial(kernel, count, heads),
        out_shape=jax.ShapeDtypeStruct(shape, queries.dtype),
        in_specs=[pl.BlockSpec(memory_space=pltpu.SMEM), hbm, hbm, hbm],
        out_specs=hbm,
        scratch_shapes=[window] * (2 * heads)
        + [pltpu.VMEM((tiles, slots, tile_len, tile_len), jnp.float32), pltpu.VMEM((tiles, tile_len, HD), jnp.float32)]
        + [pltpu.VMEM(shape, queries.dtype)] * 2
        + [pair, single, single, pair, each, pair, pair, pair, each, pair, pair],
        compiler_params=pltpu.CompilerParams(
            collective_id=0, has_side_effects=True, vmem_limit_bytes=51 * 1024 * 1024
        ),
    )(neighbours, queries.reshape(shape), keys.reshape(shape), values.reshape(shape))
    return out.reshape(tokens, width)


def solution(mesh):
    spec = P(("groups", "blk"), None)
    return jax.shard_map(
        functools.partial(on_device, mesh.shape["blk"]),
        mesh=mesh, in_specs=(spec,) * 4, out_specs=spec, check_vma=False,
    )
```

```python
import functools
import math
from typing import Any, NamedTuple

import jax
import jax.numpy as jnp
from jax import lax
from jax.experimental import pallas as pl
from jax.experimental.pallas import tpu as pltpu
from jax.sharding import PartitionSpec as P

HD = 128
WINDOW = 5
ROWS = 128


class Chunk(NamedTuple):
    index: int
    which: int
    head: int
    first: int
    rows: int
    window: Any

    @property
    def pieces(self):
        return self.rows // ROWS


def send_order(heads):
    order = [(head, which) for head in range(heads - 2) for which in range(2)]
    return order + [(heads - 2, 0), (heads - 1, 0), (heads - 2, 1), (heads - 1, 1)]


def kernel(count, heads, neighbours, queries, keys, values, out, *scratch):
    windows = scratch[: 2 * heads + 1]
    (scores, tops, rounded, totals, sums, held_q, named, named_sem, local_sem, q_sem,
     y_send, y_recv, sib_send, sib_recv, z_send, z_recv, share_send, share_recv, wide_send, ready) = scratch[2 * heads + 1 :]
    sources = (keys, values)
    tiles, tile_len, _ = queries.shape
    slots = neighbours.shape[1]
    factor = math.log2(math.e) * HD ** -0.5

    chunks = []
    for index, (head, which) in enumerate(send_order(heads)):
        first = 0
        while first < tile_len:
            left = windows[len(chunks)].shape[1]
            chunks.append(Chunk(len(chunks), which, head, first, left, windows[len(chunks)]))
            first += left

    def chunk_of(head, which):
        return [c for c in chunks if (c.head, c.which) == (head, which)]

    me = lax.axis_index("blk")
    core = lax.rem(me, 2)
    side = lax.rem(me // 2, 2)
    quad = me // 4
    last = count // 4 - 1
    sibling = me + 1 - 2 * core
    partner = me + 2 - 4 * side
    ahead = me + 4 - 8 * side
    behind = me - 4 + 8 * side
    can_relay = jnp.where(side == 0, quad < last, quad > 0)
    gets_relay = jnp.where(side == 0, quad > 0, quad < last)
    shares_partner = core == side
    sends_wide = jnp.logical_and(side == 1, jnp.logical_and(jnp.logical_not(shares_partner), quad > 0))
    gets_wide = jnp.logical_and(side == 1, jnp.logical_and(shares_partner, quad < last))
    awaits_ready = jnp.logical_and(side == 0, quad < last)
    gives_ready = jnp.logical_and(side == 0, quad > 0)
    shares_relay = jnp.logical_and(jnp.logical_not(shares_partner), gets_relay)
    partner_at = 4 - 4 * side
    relay_at = 4 * side

    def strip(head):
        return pl.ds(head * HD, HD)

    def part(c, block, piece):
        at = pl.ds(block * tiles, tiles)
        return c.window.at[at] if piece is None else c.window.at[at, pl.ds(piece * ROWS, ROWS)]

    def from_source(c, piece):
        if piece is None:
            return sources[c.which].at[:, pl.ds(c.first, c.rows), strip(c.head)]
        return sources[c.which].at[:, pl.ds(c.first + piece * ROWS, ROWS), strip(c.head)]

    def remote(src, dst, send, recv, target):
        return pltpu.make_async_remote_copy(
            src_ref=src, dst_ref=dst, send_sem=send, recv_sem=recv,
            device_id={"blk": target}, device_id_type=pl.DeviceIdType.MESH,
        )

    def partner_copy(c, piece=None):
        return remote(from_source(c, piece), part(c, relay_at, piece), y_send.at[c.index],
                      y_recv.at[c.index, 0 if piece is None else piece], partner)

    def relay_copy(c, piece=None):
        return remote(part(c, partner_at, piece), part(c, relay_at, piece), z_send.at[c.index],
                      z_recv.at[c.index, 0 if piece is None else piece], ahead)

    def share_copy(c, piece=None):
        return remote(part(c, 4 - 4 * core, piece), part(c, 3 - 2 * core, piece),
                      share_send.at[c.index], share_recv.at[c.index], sibling)

    def wide_copy(c):
        return remote(part(c, partner_at, None), part(c, 3 - 2 * core, None), wide_send,
                      share_recv.at[c.index], ahead + 1 - 2 * core)

    def own(c, tile, block):
        if tile is None:
            return from_source(c, None), part(c, block, None)
        src = sources[c.which].at[tile, pl.ds(c.first, c.rows), strip(c.head)]
        return src, c.window.at[block * tiles + tile]

    def sibling_copy(c, tile=None):
        return remote(*own(c, tile, 1 + 2 * core), sib_send.at[c.index], sib_recv.at[c.index], sibling)

    def local_copy(c, tile=None):
        return pltpu.make_async_copy(*own(c, tile, 2), local_sem.at[c.index])

    def query_copy(head, tile=None):
        at = slice(None) if tile is None else tile
        return pltpu.make_async_copy(
            queries.at[at, :, strip(head)], held_q.at[at, :, strip(head)], q_sem.at[head])

    table_copy = pltpu.make_async_copy(neighbours, named, named_sem)

    def send(c, tile):
        partner_copy(c, tile).start()
        sibling_copy(c, tile).start()
        local_copy(c, tile).start()
        if c.which == 0:
            query_copy(c.head, tile).start()

    def send_rest(c):
        for piece in range(tiles, c.pieces):
            partner_copy(c, piece).start()

    def send_short(c):
        for piece in range(c.pieces):
            partner_copy(c, piece).start()
        for tile in range(tiles):
            sibling_copy(c, tile).start()
            local_copy(c, tile).start()

    def pass_on(c, piece):
        partner_copy(c, piece).wait_recv()

        @pl.when(can_relay)
        def _():
            relay_copy(c, piece).start()

        @pl.when(shares_partner)
        def _():
            share_copy(c, piece).start()

    def share_relay(c, piece):
        @pl.when(shares_relay)
        def _():
            relay_copy(c, piece).wait_recv()
            share_copy(c, piece).start()

    def gather(c):
        local_copy(c).wait()
        sibling_copy(c).wait_recv()

        took = jnp.logical_and(side == 0, shares_relay) if c.pieces == 1 else shares_relay

        @pl.when(jnp.logical_and(gets_relay, jnp.logical_not(took)))
        def _():
            for piece in range(c.pieces):
                relay_copy(c, piece).wait_recv()

        @pl.when(jnp.logical_or(jnp.logical_not(shares_partner), gets_relay))
        def _():
            share_copy(c).wait_recv()

    def drain(c):
        partner_copy(c).wait_send()
        sibling_copy(c).wait_send()

        @pl.when(can_relay)
        def _():
            relay_copy(c).wait_send()

        passed = jnp.logical_and(side == 0, shares_relay) if c.pieces == 1 else shares_relay

        @pl.when(jnp.logical_or(shares_partner, passed))
        def _():
            share_copy(c).wait_send()

    def place_of(tile, slot):
        entry = named[tile, slot]
        ok = entry >= 0
        place = jnp.where(ok, entry - (me - 2) * tiles, 2 * tiles + tile)
        return ok, jnp.clip(place, 0, WINDOW * tiles - 1)

    def score(head, tile, room):
        (c,) = chunk_of(head, 0)
        query = held_q[tile, :, strip(head)]
        peak = None
        for slot in range(slots):
            score = lax.dot_general(
                query, c.window[place_of(tile, slot)[1]], (((1,), (1,)), ((), ())),
                preferred_element_type=jnp.float32,
            )
            scores[room, slot] = score
            for lane in range(0, tile_len, HD):
                lanes = score[:, lane : lane + HD]
                peak = lanes if peak is None else jnp.maximum(peak, lanes)
        top = jnp.max(peak, axis=1, keepdims=True) * factor
        tops[room] = jnp.broadcast_to(top, tops.shape[1:])

    def weigh(room, slot, ok):
        offset = jnp.where(ok, tops[room, :, 0:1], jnp.inf)
        return jnp.exp2(scores[room, slot] * factor - offset)

    def mix(head, tile):
        (c,) = chunk_of(head, 1)
        total = jnp.zeros((tile_len, HD), jnp.float32)
        summed = jnp.zeros((tile_len, HD), jnp.float32)
        for slot in range(slots):
            ok, place = place_of(tile, slot)
            weights = weigh(tile, slot, ok)
            for lane in range(0, tile_len, HD):
                total += weights[:, lane : lane + HD]
            summed += jnp.dot(
                weights.astype(jnp.bfloat16), c.window[place], preferred_element_type=jnp.float32)
        out[tile, :, strip(head)] = (summed / jnp.sum(total, axis=1, keepdims=True)).astype(out.dtype)

    def settle(tile, room):
        total = jnp.zeros((tile_len, HD), jnp.float32)
        for slot in range(slots):
            ok, _ = place_of(tile, slot)
            weights = weigh(room, slot, ok)
            for lane in range(0, tile_len, HD):
                total += weights[:, lane : lane + HD]
            rounded[tile, slot] = weights.astype(jnp.bfloat16)
        totals[tile] = jnp.broadcast_to(jnp.sum(total, axis=1, keepdims=True), totals.shape[1:])

    def collect(c, tile):
        summed = jnp.zeros((tile_len, HD), jnp.float32)
        for slot in range(slots):
            _, place = place_of(tile, slot)
            summed += jnp.dot(
                rounded[tile, slot, :, c.first : c.first + c.rows], c.window[place],
                preferred_element_type=jnp.float32)
        return summed

    barrier = pltpu.get_barrier_semaphore()

    def greet(target):
        pl.semaphore_signal(barrier, inc=1, device_id={"blk": target}, device_id_type=pl.DeviceIdType.MESH)

    greet(partner)
    greet(sibling)

    @pl.when(quad < last)
    def _():
        greet(me + 4)

    @pl.when(gets_wide)
    def _():
        greet(me + 5 - 2 * core)

    pl.semaphore_wait(barrier, 2 + (quad > 0).astype(jnp.int32) + sends_wide.astype(jnp.int32))

    whole = [c for c in chunks if c.rows == tile_len]
    first_part, last_part = chunks[len(whole) :]
    final = heads - 1
    (final_keys,) = chunk_of(final, 0)
    (late_values,) = chunk_of(final - 1, 1)

    for c in chunks[:2]:
        for tile in range(tiles):
            send(c, tile)
        send_rest(c)
        if c.index == 0:
            table_copy.start()
    ordered = [(head, which) for head in range(heads - 2) for which in range(2)]

    @pl.when(gives_ready)
    def _():
        pl.semaphore_signal(ready, inc=1, device_id={"blk": behind}, device_id_type=pl.DeviceIdType.MESH)

    @pl.when(awaits_ready)
    def _():
        pl.semaphore_wait(ready, 1)

    for c in chunks[:-3]:
        task = ordered[c.index - 2] if c.index >= 2 else None

        pass_on(c, 0)
        if c.index > 0:
            share_relay(chunks[c.index - 1], 0)

        @pl.loop(0, tiles)
        def _(tile):
            pass_on(c, tile + 1)
            if c.index > 0:
                share_relay(chunks[c.index - 1], tile + 1)
            send(chunks[c.index + 2], tile)
            if task:
                @pl.when(tile == 0)
                def _():
                    if c.index == 2:
                        table_copy.wait()
                    if task[1] == 0:
                        query_copy(task[0]).wait()
                    gather(*chunk_of(*task))

                if task[1] == 0:
                    score(task[0], tile, tile)
                else:
                    mix(task[0], tile)

        send_rest(chunks[c.index + 2])
        if c.index + 2 == first_part.index:
            send_short(last_part)
        if c.index >= 2:
            drain(chunks[c.index - 2])

    pass_on(late_values, 0)
    share_relay(final_keys, 0)

    @pl.loop(0, tiles)
    def _(tile):
        pass_on(late_values, tile + 1)
        share_relay(final_keys, tile + 1)

        @pl.when(tile == 0)
        def _():
            query_copy(final - 1).wait()
            gather(*chunk_of(final - 1, 0))

        score(final - 1, tile, tile)

    drain(chunks[late_values.index - 2])
    pass_on(first_part, 0)
    share_relay(late_values, 0)
    query_copy(final).wait()
    gather(final_keys)

    @pl.loop(0, tiles)
    def _(tile):
        score(final, tile, tiles)

        @pl.when(tile == 0)
        def _():
            pass_on(first_part, 1)
            share_relay(late_values, 1)

        settle(tile, tiles)

        @pl.when(tile == 0)
        def _():
            pass_on(last_part, 0)

            @pl.when(sends_wide)
            def _():
                wide_copy(last_part).start()

            share_relay(late_values, 2)

    share_relay(first_part, 0)
    gather(late_values)

    @pl.loop(0, tiles)
    def _(tile):
        mix(final - 1, tile)

        @pl.when(tile == 0)
        def _():
            share_relay(first_part, 1)

        @pl.when(jnp.logical_and(tile == 1, side == 0))
        def _():
            share_relay(last_part, 0)

    drain(chunks[late_values.index - 1])
    drain(late_values)
    gather(first_part)

    @pl.loop(0, tiles)
    def _(tile):
        sums[tile] = collect(first_part, tile)

    gather(last_part)

    @pl.loop(0, tiles)
    def _(tile):
        summed = sums[tile] + collect(last_part, tile)
        out[tile, :, strip(final)] = (summed / totals[tile]).astype(out.dtype)

    drain(first_part)
    drain(last_part)

    @pl.when(sends_wide)
    def _():
        wide_copy(last_part).wait_send()


def on_device(count, queries, keys, values, neighbours):
    tokens, width = queries.shape
    tiles, slots = neighbours.shape
    tile_len = tokens // tiles
    heads = width // HD
    shape = (tiles, tile_len, width)
    lengths = [tile_len] * (2 * heads - 1) + [tile_len - ROWS, ROWS]
    windows = [pltpu.VMEM((WINDOW * tiles, length, HD), queries.dtype) for length in lengths]
    column = pltpu.VMEM((tiles, tile_len, HD), jnp.float32)
    per_chunk = pltpu.SemaphoreType.DMA((len(lengths),))
    per_piece = pltpu.SemaphoreType.DMA((len(lengths), tile_len // ROWS))
    hbm = pl.BlockSpec(memory_space=pl.ANY)
    neighbours = pltpu.with_memory_space_constraint(neighbours, pltpu.HBM)
    out = pl.pallas_call(
        functools.partial(kernel, count, heads),
        out_shape=jax.ShapeDtypeStruct(shape, queries.dtype),
        in_specs=[hbm, hbm, hbm, hbm],
        out_specs=pl.BlockSpec(memory_space=pltpu.VMEM),
        scratch_shapes=windows
        + [
            pltpu.VMEM((tiles + 1, slots, tile_len, tile_len), jnp.float32),
            pltpu.VMEM((tiles + 1, tile_len, HD), jnp.float32),
            pltpu.VMEM((tiles, slots, tile_len, tile_len), jnp.bfloat16),
            column,
            column,
            pltpu.VMEM(shape, queries.dtype),
            pltpu.SMEM((tiles, slots), jnp.int32),
            pltpu.SemaphoreType.DMA,
            per_chunk,
            pltpu.SemaphoreType.DMA((heads,)),
        ]
        + [per_chunk, per_piece, per_chunk, per_chunk, per_chunk, per_piece, per_chunk, per_chunk]
        + [pltpu.SemaphoreType.DMA, pltpu.SemaphoreType.REGULAR],
        compiler_params=pltpu.CompilerParams(
            collective_id=0, has_side_effects=True, vmem_limit_bytes=51 * 1024 * 1024
        ),
    )(neighbours, queries.reshape(shape), keys.reshape(shape), values.reshape(shape))
    return out.reshape(tokens, width)


def solution(mesh):
    spec = P(("groups", "blk"), None)
    return jax.shard_map(
        functools.partial(on_device, mesh.shape["blk"]),
        mesh=mesh, in_specs=(spec,) * 4, out_specs=spec, check_vma=False,
    )
```

```python
import functools
import math
from typing import Any, NamedTuple

import jax
import jax.numpy as jnp
from jax import lax
from jax.experimental import pallas as pl
from jax.experimental.pallas import tpu as pltpu
from jax.sharding import PartitionSpec as P

HD = 128
WINDOW = 5
ROWS = 128
SENDS = 6
LANDS = 10
SHARES = 8
QUERIES = 4


class Chunk(NamedTuple):
    index: int
    which: int
    head: int
    first: int
    rows: int
    window: Any

    @property
    def pieces(self):
        return self.rows // ROWS


def send_order(heads):
    order = [(head, which) for head in range(heads - 2) for which in range(2)]
    return order + [(heads - 1, 0), (heads - 2, 0), (heads - 2, 1), (heads - 1, 1)]


def kernel(count, heads, neighbours, queries, keys, values, out, *scratch):
    windows = scratch[: 2 * heads + 1]
    (scores, tops, rounded_first, rounded_last, gathered_first, gathered_last, totals, sums, held_q, named, named_sem, local_sem, q_sem,
     y_send, y_recv, sib_send, sib_recv, z_send, z_recv, share_send, share_recv, wide_send, ready) = scratch[2 * heads + 1 :]
    sources = (keys, values)
    rounded, gathered = (rounded_first, rounded_last), (gathered_first, gathered_last)
    tiles, tile_len, _ = queries.shape
    slots = neighbours.shape[1]
    factor = math.log2(math.e) * HD ** -0.5

    chunks = []
    for index, (head, which) in enumerate(send_order(heads)):
        first = 0
        while first < tile_len:
            left = windows[len(chunks)].shape[1]
            chunks.append(Chunk(len(chunks), which, head, first, left, windows[len(chunks)]))
            first += left

    def chunk_of(head, which):
        return [c for c in chunks if (c.head, c.which) == (head, which)]

    me = lax.axis_index("blk")
    core = lax.rem(me, 2)
    side = lax.rem(me // 2, 2)
    quad = me // 4
    last = count // 4 - 1
    sibling = me + 1 - 2 * core
    partner = me + 2 - 4 * side
    ahead = me + 4 - 8 * side
    behind = me - 4 + 8 * side
    can_relay = jnp.where(side == 0, quad < last, quad > 0)
    gets_relay = jnp.where(side == 0, quad > 0, quad < last)
    shares_partner = core == side
    sends_wide = jnp.logical_and(side == 1, jnp.logical_and(jnp.logical_not(shares_partner), quad > 0))
    gets_wide = jnp.logical_and(side == 1, jnp.logical_and(shares_partner, quad < last))
    awaits_ready = jnp.logical_and(side == 0, quad < last)
    gives_ready = jnp.logical_and(side == 0, quad > 0)
    shares_relay = jnp.logical_and(jnp.logical_not(shares_partner), gets_relay)
    partner_at = 4 - 4 * side
    relay_at = 4 * side

    def strip(head):
        return pl.ds(head * HD, HD)

    def part(c, block, piece):
        at = pl.ds(block * tiles, tiles)
        return c.window.at[at] if piece is None else c.window.at[at, pl.ds(piece * ROWS, ROWS)]

    def from_source(c, piece):
        if piece is None:
            return sources[c.which].at[:, pl.ds(c.first, c.rows), strip(c.head)]
        return sources[c.which].at[:, pl.ds(c.first + piece * ROWS, ROWS), strip(c.head)]

    def remote(src, dst, send, recv, target):
        return pltpu.make_async_remote_copy(
            src_ref=src, dst_ref=dst, send_sem=send, recv_sem=recv,
            device_id={"blk": target}, device_id_type=pl.DeviceIdType.MESH,
        )

    def partner_copy(c, piece=None):
        return remote(from_source(c, piece), part(c, relay_at, piece), y_send.at[c.index % SENDS],
                      y_recv.at[c.index % SENDS, 0 if piece is None else piece], partner)

    def relay_copy(c, piece=None):
        return remote(part(c, partner_at, piece), part(c, relay_at, piece), z_send.at[c.index % SENDS],
                      z_recv.at[c.index % LANDS, 0 if piece is None else piece], ahead)

    def share_slot(c):
        return SHARES if c.pieces == 1 else c.index % SHARES

    def share_copy(c, piece=None):
        return remote(part(c, 4 - 4 * core, piece), part(c, 3 - 2 * core, piece),
                      share_send.at[c.index % SENDS], share_recv.at[share_slot(c)], sibling)

    def wide_copy(c):
        return remote(part(c, partner_at, None), part(c, 3 - 2 * core, None), wide_send,
                      share_recv.at[share_slot(c)], ahead + 1 - 2 * core)

    def own(c, tile, block):
        if tile is None:
            return from_source(c, None), part(c, block, None)
        src = sources[c.which].at[tile, pl.ds(c.first, c.rows), strip(c.head)]
        return src, c.window.at[block * tiles + tile]

    def sibling_copy(c, tile=None):
        return remote(*own(c, tile, 1 + 2 * core), sib_send.at[c.index % SENDS], sib_recv.at[c.index % LANDS], sibling)

    def local_copy(c, tile=None):
        return pltpu.make_async_copy(*own(c, tile, 2), local_sem.at[c.index % SENDS])

    def query_copy(head, tile=None):
        at = slice(None) if tile is None else tile
        return pltpu.make_async_copy(
            queries.at[at, :, strip(head)], held_q.at[at, :, strip(head)], q_sem.at[head % QUERIES])

    table_copy = pltpu.make_async_copy(neighbours, named, named_sem)

    def send(c, tile):
        partner_copy(c, tile).start()
        sibling_copy(c, tile).start()
        local_copy(c, tile).start()
        if c.which == 0:
            query_copy(c.head, tile).start()

    def send_rest(c):
        for piece in range(tiles, c.pieces):
            partner_copy(c, piece).start()

    def send_short(c):
        for piece in range(c.pieces):
            partner_copy(c, piece).start()
        for tile in range(tiles):
            sibling_copy(c, tile).start()
            local_copy(c, tile).start()

    def pass_on(c, piece):
        partner_copy(c, piece).wait_recv()

        @pl.when(can_relay)
        def _():
            relay_copy(c, piece).start()

        @pl.when(shares_partner)
        def _():
            share_copy(c, piece).start()

    def share_relay(c, piece):
        @pl.when(shares_relay)
        def _():
            relay_copy(c, piece).wait_recv()
            share_copy(c, piece).start()

    def gather(c):
        local_copy(c).wait()
        sibling_copy(c).wait_recv()

        took = jnp.logical_and(side == 0, shares_relay) if c.pieces == 1 else shares_relay

        @pl.when(jnp.logical_and(gets_relay, jnp.logical_not(took)))
        def _():
            for piece in range(c.pieces):
                relay_copy(c, piece).wait_recv()

        @pl.when(jnp.logical_or(jnp.logical_not(shares_partner), gets_relay))
        def _():
            share_copy(c).wait_recv()

    def drain(c):
        partner_copy(c).wait_send()
        sibling_copy(c).wait_send()

        @pl.when(can_relay)
        def _():
            relay_copy(c).wait_send()

        passed = jnp.logical_and(side == 0, shares_relay) if c.pieces == 1 else shares_relay

        @pl.when(jnp.logical_or(shares_partner, passed))
        def _():
            share_copy(c).wait_send()

    def place_of(tile, slot):
        entry = named[tile, slot]
        ok = entry >= 0
        place = jnp.where(ok, entry - (me - 2) * tiles, 2 * tiles + tile)
        return ok, jnp.clip(place, 0, WINDOW * tiles - 1)

    def score(head, tile, room):
        (c,) = chunk_of(head, 0)
        query = held_q[tile, :, strip(head)]
        peak = None
        for slot in range(slots):
            score = lax.dot_general(
                query, c.window[place_of(tile, slot)[1]], (((1,), (1,)), ((), ())),
                preferred_element_type=jnp.float32,
            )
            scores[room, slot] = score
            for lane in range(0, tile_len, HD):
                lanes = score[:, lane : lane + HD]
                peak = lanes if peak is None else jnp.maximum(peak, lanes)
        top = jnp.max(peak, axis=1, keepdims=True) * factor
        tops[room] = jnp.broadcast_to(top, tops.shape[1:])

    def weigh(room, slot, ok):
        offset = jnp.where(ok, tops[room, :, 0:1], jnp.inf)
        return jnp.exp2(scores[room, slot] * factor - offset)

    def mix(head, tile):
        (c,) = chunk_of(head, 1)
        total = jnp.zeros((tile_len, HD), jnp.float32)
        summed = jnp.zeros((tile_len, HD), jnp.float32)
        for slot in range(slots):
            ok, place = place_of(tile, slot)
            weights = weigh(tile, slot, ok)
            for lane in range(0, tile_len, HD):
                total += weights[:, lane : lane + HD]
            summed += jnp.dot(
                weights.astype(jnp.bfloat16), c.window[place], preferred_element_type=jnp.float32)
        out[tile, :, strip(head)] = (summed / jnp.sum(total, axis=1, keepdims=True)).astype(out.dtype)

    def settle(tile, room):
        total = jnp.zeros((tile_len, HD), jnp.float32)
        for slot in range(slots):
            ok, _ = place_of(tile, slot)
            weights = weigh(room, slot, ok)
            for lane in range(0, tile_len, HD):
                total += weights[:, lane : lane + HD]
            weights = weights.astype(jnp.bfloat16)
            for ref, c in zip(rounded, chunks[-2:]):
                ref[tile, :, slot * c.rows : (slot + 1) * c.rows] = weights[:, c.first : c.first + c.rows]
        totals[tile] = jnp.broadcast_to(jnp.sum(total, axis=1, keepdims=True), totals.shape[1:])

    def collect(part, tile):
        c, held = chunks[part - 2], gathered[part]
        for slot in range(slots):
            held[slot * c.rows : (slot + 1) * c.rows] = c.window[place_of(tile, slot)[1]]
        return jnp.dot(rounded[part][tile], held[...], preferred_element_type=jnp.float32)

    barrier = pltpu.get_barrier_semaphore()

    def greet(target):
        pl.semaphore_signal(barrier, inc=1, device_id={"blk": target}, device_id_type=pl.DeviceIdType.MESH)

    greet(partner)
    greet(sibling)

    @pl.when(quad < last)
    def _():
        greet(me + 4)

    @pl.when(gets_wide)
    def _():
        greet(me + 5 - 2 * core)

    pl.semaphore_wait(barrier, 2 + (quad > 0).astype(jnp.int32) + sends_wide.astype(jnp.int32))

    whole = [c for c in chunks if c.rows == tile_len]
    first_part, last_part = chunks[len(whole) :]
    final = heads - 1
    (final_keys,) = chunk_of(final, 0)
    (late_keys,) = chunk_of(final - 1, 0)
    (late_values,) = chunk_of(final - 1, 1)

    for piece in range(chunks[0].pieces):
        partner_copy(chunks[0], piece).start()
    for tile in range(tiles):
        sibling_copy(chunks[0], tile).start()
        local_copy(chunks[0], tile).start()
        query_copy(0, tile).start()
    table_copy.start()
    for tile in range(tiles):
        send(chunks[1], tile)
    send_rest(chunks[1])
    ordered = [(head, which) for head in range(heads - 2) for which in range(2)]

    @pl.when(gives_ready)
    def _():
        pl.semaphore_signal(ready, inc=1, device_id={"blk": behind}, device_id_type=pl.DeviceIdType.MESH)

    @pl.when(awaits_ready)
    def _():
        pl.semaphore_wait(ready, 1)

    for c in chunks[:-3]:
        task = ordered[c.index - 2] if c.index >= 2 else None

        pass_on(c, 0)
        if c.index > 0:
            share_relay(chunks[c.index - 1], 0)

        @pl.loop(0, tiles)
        def _(tile):
            pass_on(c, tile + 1)
            if c.index > 0:
                share_relay(chunks[c.index - 1], tile + 1)
            send(chunks[c.index + 2], tile)
            if task:
                @pl.when(tile == 0)
                def _():
                    if c.index == 2:
                        table_copy.wait()
                    if task[1] == 0:
                        query_copy(task[0]).wait()
                    gather(*chunk_of(*task))

                if task[1] == 0:
                    score(task[0], tile, tile)
                else:
                    mix(task[0], tile)

        send_rest(chunks[c.index + 2])
        if c.index + 2 == first_part.index:
            send_short(last_part)
        if c.index >= 2:
            drain(chunks[c.index - 2])

    pass_on(late_values, 0)
    share_relay(late_keys, 0)
    query_copy(final).wait()
    gather(final_keys)

    @pl.loop(0, tiles)
    def _(tile):
        score(final, tile, tiles)

        @pl.when(tile == 0)
        def _():
            pass_on(late_values, 1)
            share_relay(late_keys, 1)

        @pl.when(tile == 1)
        def _():
            pass_on(first_part, 0)
            share_relay(late_values, 0)

        settle(tile, tiles)

        @pl.when(tile == 0)
        def _():
            pass_on(late_values, 2)
            share_relay(late_keys, 2)

    drain(final_keys)
    query_copy(final - 1).wait()
    gather(late_keys)
    pass_on(first_part, 1)
    share_relay(late_values, 1)

    @pl.loop(0, tiles)
    def _(tile):
        score(final - 1, tile, tile)

        @pl.when(tile == 0)
        def _():
            pass_on(last_part, 0)

            @pl.when(sends_wide)
            def _():
                wide_copy(last_part).start()

            share_relay(late_values, 2)

    share_relay(first_part, 0)
    gather(late_values)

    @pl.loop(0, tiles)
    def _(tile):
        mix(final - 1, tile)

        @pl.when(tile == 0)
        def _():
            share_relay(first_part, 1)

        @pl.when(jnp.logical_and(tile == 1, side == 0))
        def _():
            share_relay(last_part, 0)

    drain(late_keys)
    drain(late_values)
    gather(first_part)

    @pl.loop(0, tiles)
    def _(tile):
        sums[tile] = collect(0, tile)

    gather(last_part)

    @pl.loop(0, tiles)
    def _(tile):
        summed = sums[tile] + collect(1, tile)
        out[tile, :, strip(final)] = (summed / totals[tile]).astype(out.dtype)

    drain(first_part)
    drain(last_part)

    @pl.when(sends_wide)
    def _():
        wide_copy(last_part).wait_send()


def on_device(count, queries, keys, values, neighbours):
    tokens, width = queries.shape
    tiles, slots = neighbours.shape
    tile_len = tokens // tiles
    heads = width // HD
    shape = (tiles, tile_len, width)
    lengths = [tile_len] * (2 * heads - 1) + [tile_len - ROWS, ROWS]
    windows = [pltpu.VMEM((WINDOW * tiles, length, HD), queries.dtype) for length in lengths]
    column = pltpu.VMEM((tiles, tile_len, HD), jnp.float32)
    pieces = tile_len // ROWS
    sends = pltpu.SemaphoreType.DMA((SENDS,))
    hbm = pl.BlockSpec(memory_space=pl.ANY)
    neighbours = pltpu.with_memory_space_constraint(neighbours, pltpu.HBM)
    out = pl.pallas_call(
        functools.partial(kernel, count, heads),
        out_shape=jax.ShapeDtypeStruct(shape, queries.dtype),
        in_specs=[hbm, hbm, hbm, hbm],
        out_specs=pl.BlockSpec(memory_space=pltpu.VMEM),
        scratch_shapes=windows
        + [
            pltpu.VMEM((tiles + 1, slots, tile_len, tile_len), jnp.float32),
            pltpu.VMEM((tiles + 1, tile_len, HD), jnp.float32),
            pltpu.VMEM((tiles, tile_len, slots * lengths[-2]), jnp.bfloat16),
            pltpu.VMEM((tiles, tile_len, slots * lengths[-1]), jnp.bfloat16),
            pltpu.VMEM((slots * lengths[-2], HD), queries.dtype),
            pltpu.VMEM((slots * lengths[-1], HD), queries.dtype),
            column,
            column,
            pltpu.VMEM(shape, queries.dtype),
            pltpu.SMEM((tiles, slots), jnp.int32),
            pltpu.SemaphoreType.DMA,
            sends,
            pltpu.SemaphoreType.DMA((QUERIES,)),
        ]
        + [sends, pltpu.SemaphoreType.DMA((SENDS, pieces)), sends, pltpu.SemaphoreType.DMA((LANDS,))]
        + [sends, pltpu.SemaphoreType.DMA((LANDS, pieces)), sends, pltpu.SemaphoreType.DMA((SHARES + 1,))]
        + [pltpu.SemaphoreType.DMA, pltpu.SemaphoreType.REGULAR],
        compiler_params=pltpu.CompilerParams(
            collective_id=0, has_side_effects=True, vmem_limit_bytes=51 * 1024 * 1024
        ),
    )(neighbours, queries.reshape(shape), keys.reshape(shape), values.reshape(shape))
    return out.reshape(tokens, width)


def solution(mesh):
    spec = P(("groups", "blk"), None)
    return jax.shard_map(
        functools.partial(on_device, mesh.shape["blk"]),
        mesh=mesh, in_specs=(spec,) * 4, out_specs=spec, check_vma=False,
    )
```

```python
import functools
import math
from typing import Any, NamedTuple

import jax
import jax.numpy as jnp
from jax import lax
from jax.experimental import pallas as pl
from jax.experimental.pallas import tpu as pltpu
from jax.sharding import PartitionSpec as P

HD = 128
WINDOW = 5
ROWS = 128
SENDS = 5
LANDS = 9
SHARES = 7
RELAYS = 4
QUERIES = 4


class Chunk(NamedTuple):
    index: int
    which: int
    head: int
    first: int
    rows: int
    window: Any

    @property
    def pieces(self):
        return self.rows // ROWS


def send_order(heads):
    order = [(head, which) for head in range(heads - 2) for which in range(2)]
    return order + [(heads - 1, 0), (heads - 2, 0), (heads - 2, 1), (heads - 1, 1)]


def kernel(count, heads, neighbours, queries, keys, values, out, *scratch):
    windows = scratch[: 2 * heads + 1]
    (scores, tops, rounded_first, rounded_last, gathered_first, gathered_last, totals, sums, held_q, named, named_sem, local_sem, q_sem,
     y_send, y_recv, sib_send, sib_recv, z_send, z_recv, share_send, share_recv, wide_send, ready) = scratch[2 * heads + 1 :]
    sources = (keys, values)
    rounded, gathered = (rounded_first, rounded_last), (gathered_first, gathered_last)
    tiles, tile_len, _ = queries.shape
    slots = neighbours.shape[1]
    factor = math.log2(math.e) * HD ** -0.5

    chunks = []
    for index, (head, which) in enumerate(send_order(heads)):
        first = 0
        while first < tile_len:
            left = windows[len(chunks)].shape[1]
            chunks.append(Chunk(len(chunks), which, head, first, left, windows[len(chunks)]))
            first += left

    def chunk_of(head, which):
        return [c for c in chunks if (c.head, c.which) == (head, which)]

    me = lax.axis_index("blk")
    core = lax.rem(me, 2)
    side = lax.rem(me // 2, 2)
    quad = me // 4
    last = count // 4 - 1
    sibling = me + 1 - 2 * core
    partner = me + 2 - 4 * side
    ahead = me + 4 - 8 * side
    behind = me - 4 + 8 * side
    can_relay = jnp.where(side == 0, quad < last, quad > 0)
    gets_relay = jnp.where(side == 0, quad > 0, quad < last)
    shares_partner = core == side
    sends_wide = count < 0
    gets_wide = count < 0
    awaits_ready = jnp.logical_and(side == 0, quad < last)
    gives_ready = jnp.logical_and(side == 0, quad > 0)
    shares_relay = jnp.logical_and(jnp.logical_not(shares_partner), gets_relay)
    partner_at = 4 - 4 * side
    relay_at = 4 * side

    def strip(head):
        return pl.ds(head * HD, HD)

    def part(c, block, piece):
        at = pl.ds(block * tiles, tiles)
        return c.window.at[at] if piece is None else c.window.at[at, pl.ds(piece * ROWS, ROWS)]

    def from_source(c, piece):
        if piece is None:
            return sources[c.which].at[:, pl.ds(c.first, c.rows), strip(c.head)]
        return sources[c.which].at[:, pl.ds(c.first + piece * ROWS, ROWS), strip(c.head)]

    def remote(src, dst, send, recv, target):
        return pltpu.make_async_remote_copy(
            src_ref=src, dst_ref=dst, send_sem=send, recv_sem=recv,
            device_id={"blk": target}, device_id_type=pl.DeviceIdType.MESH,
        )

    def partner_copy(c, piece=None):
        return remote(from_source(c, piece), part(c, relay_at, piece), y_send.at[c.index % SENDS],
                      y_recv.at[c.index % SENDS, 0 if piece is None else piece], partner)

    def relay_copy(c, piece=None):
        return remote(part(c, partner_at, piece), part(c, relay_at, piece), z_send.at[c.index % RELAYS],
                      z_recv.at[c.index % LANDS, 0 if piece is None else piece], ahead)

    def share_slot(c):
        return SHARES if c.pieces == 1 else c.index % SHARES

    def share_copy(c, piece=None):
        return remote(part(c, 4 - 4 * core, piece), part(c, 3 - 2 * core, piece),
                      share_send.at[c.index % RELAYS], share_recv.at[share_slot(c)], sibling)

    def wide_copy(c):
        return remote(part(c, partner_at, None), part(c, 3 - 2 * core, None), wide_send,
                      share_recv.at[share_slot(c)], ahead + 1 - 2 * core)

    def own(c, tile, block):
        if tile is None:
            return from_source(c, None), part(c, block, None)
        src = sources[c.which].at[tile, pl.ds(c.first, c.rows), strip(c.head)]
        return src, c.window.at[block * tiles + tile]

    def sibling_copy(c, tile=None):
        return remote(*own(c, tile, 1 + 2 * core), sib_send.at[c.index % SENDS], sib_recv.at[c.index % LANDS], sibling)

    def local_copy(c, tile=None):
        return pltpu.make_async_copy(*own(c, tile, 2), local_sem.at[c.index % SENDS])

    def query_copy(head, tile=None):
        at = slice(None) if tile is None else tile
        return pltpu.make_async_copy(
            queries.at[at, :, strip(head)], held_q.at[at, :, strip(head)], q_sem.at[head % QUERIES])

    table_copy = pltpu.make_async_copy(neighbours, named, named_sem)

    def send(c, tile):
        partner_copy(c, tile).start()
        sibling_copy(c, tile).start()
        local_copy(c, tile).start()
        if c.which == 0:
            query_copy(c.head, tile).start()

    def send_rest(c):
        for piece in range(tiles, c.pieces):
            partner_copy(c, piece).start()

    def send_short(c):
        for piece in range(c.pieces):
            partner_copy(c, piece).start()
        for tile in range(tiles):
            sibling_copy(c, tile).start()
            local_copy(c, tile).start()

    def pass_on(c, piece):
        partner_copy(c, piece).wait_recv()

        @pl.when(can_relay)
        def _():
            relay_copy(c, piece).start()

        @pl.when(shares_partner)
        def _():
            share_copy(c, piece).start()

    def share_relay(c, piece):
        @pl.when(shares_relay)
        def _():
            relay_copy(c, piece).wait_recv()
            share_copy(c, piece).start()

    def gather(c):
        local_copy(c).wait()
        sibling_copy(c).wait_recv()

        took = shares_relay

        @pl.when(jnp.logical_and(gets_relay, jnp.logical_not(took)))
        def _():
            for piece in range(c.pieces):
                relay_copy(c, piece).wait_recv()

        @pl.when(jnp.logical_or(jnp.logical_not(shares_partner), gets_relay))
        def _():
            share_copy(c).wait_recv()

    def drain(c):
        partner_copy(c).wait_send()
        sibling_copy(c).wait_send()

        @pl.when(can_relay)
        def _():
            relay_copy(c).wait_send()

        passed = shares_relay

        @pl.when(jnp.logical_or(shares_partner, passed))
        def _():
            share_copy(c).wait_send()

    def place_of(tile, slot):
        entry = named[tile, slot]
        ok = entry >= 0
        place = jnp.where(ok, entry - (me - 2) * tiles, 2 * tiles + tile)
        return ok, jnp.clip(place, 0, WINDOW * tiles - 1)

    def score(head, tile, room):
        (c,) = chunk_of(head, 0)
        query = held_q[tile, :, strip(head)]
        peak = None
        for slot in range(slots):
            score = lax.dot_general(
                query, c.window[place_of(tile, slot)[1]], (((1,), (1,)), ((), ())),
                preferred_element_type=jnp.float32,
            )
            scores[room, slot] = score
            for lane in range(0, tile_len, HD):
                lanes = score[:, lane : lane + HD]
                peak = lanes if peak is None else jnp.maximum(peak, lanes)
        top = jnp.max(peak, axis=1, keepdims=True) * factor
        tops[room] = jnp.broadcast_to(top, tops.shape[1:])

    def weigh(room, slot, ok):
        offset = jnp.where(ok, tops[room, :, 0:1], jnp.inf)
        return jnp.exp2(scores[room, slot] * factor - offset)

    def mix(head, tile):
        (c,) = chunk_of(head, 1)
        total = jnp.zeros((tile_len, HD), jnp.float32)
        summed = jnp.zeros((tile_len, HD), jnp.float32)
        for slot in range(slots):
            ok, place = place_of(tile, slot)
            weights = weigh(tile, slot, ok)
            for lane in range(0, tile_len, HD):
                total += weights[:, lane : lane + HD]
            summed += jnp.dot(
                weights.astype(jnp.bfloat16), c.window[place], preferred_element_type=jnp.float32)
        out[tile, :, strip(head)] = (summed / jnp.sum(total, axis=1, keepdims=True)).astype(out.dtype)

    def settle(tile, room):
        total = jnp.zeros((tile_len, HD), jnp.float32)
        for slot in range(slots):
            ok, _ = place_of(tile, slot)
            weights = weigh(room, slot, ok)
            for lane in range(0, tile_len, HD):
                total += weights[:, lane : lane + HD]
            weights = weights.astype(jnp.bfloat16)
            for ref, c in zip(rounded, chunks[-2:]):
                ref[tile, :, slot * c.rows : (slot + 1) * c.rows] = weights[:, c.first : c.first + c.rows]
        totals[tile] = jnp.broadcast_to(jnp.sum(total, axis=1, keepdims=True), totals.shape[1:])

    def collect(part, tile):
        c, held = chunks[part - 2], gathered[part]
        for slot in range(slots):
            held[slot * c.rows : (slot + 1) * c.rows] = c.window[place_of(tile, slot)[1]]
        return jnp.dot(rounded[part][tile], held[...], preferred_element_type=jnp.float32)

    barrier = pltpu.get_barrier_semaphore()

    def greet(target):
        pl.semaphore_signal(barrier, inc=1, device_id={"blk": target}, device_id_type=pl.DeviceIdType.MESH)

    greet(partner)
    greet(sibling)

    @pl.when(quad < last)
    def _():
        greet(me + 4)

    pl.semaphore_wait(barrier, 2 + (quad > 0).astype(jnp.int32) )

    whole = [c for c in chunks if c.rows == tile_len]
    first_part, last_part = chunks[len(whole) :]
    final = heads - 1
    (final_keys,) = chunk_of(final, 0)
    (late_keys,) = chunk_of(final - 1, 0)
    (late_values,) = chunk_of(final - 1, 1)

    for piece in range(chunks[0].pieces):
        partner_copy(chunks[0], piece).start()
    for tile in range(tiles):
        sibling_copy(chunks[0], tile).start()
        local_copy(chunks[0], tile).start()
        query_copy(0, tile).start()
    table_copy.start()
    for tile in range(tiles):
        send(chunks[1], tile)
    send_rest(chunks[1])
    ordered = [(head, which) for head in range(heads - 2) for which in range(2)]

    @pl.when(gives_ready)
    def _():
        pl.semaphore_signal(ready, inc=1, device_id={"blk": behind}, device_id_type=pl.DeviceIdType.MESH)

    @pl.when(awaits_ready)
    def _():
        pl.semaphore_wait(ready, 1)

    for c in chunks[:-3]:
        task = ordered[c.index - 2] if c.index >= 2 else None

        pass_on(c, 0)
        if c.index > 0:
            share_relay(chunks[c.index - 1], 0)

        @pl.loop(0, tiles)
        def _(tile):
            pass_on(c, tile + 1)
            if c.index > 0:
                share_relay(chunks[c.index - 1], tile + 1)
            send(chunks[c.index + 2], tile)
            if task:
                @pl.when(tile == 0)
                def _():
                    if c.index == 2:
                        table_copy.wait()
                    if task[1] == 0:
                        query_copy(task[0]).wait()
                    gather(*chunk_of(*task))

                if task[1] == 0:
                    score(task[0], tile, tile)
                else:
                    mix(task[0], tile)

        send_rest(chunks[c.index + 2])
        if c.index >= 2:
            drain(chunks[c.index - 2])
        if c.index + 2 == first_part.index:
            send_short(last_part)

    pass_on(late_values, 0)
    share_relay(late_keys, 0)
    query_copy(final).wait()
    gather(final_keys)

    @pl.loop(0, tiles)
    def _(tile):
        score(final, tile, tiles)

        @pl.when(tile == 0)
        def _():
            pass_on(late_values, 1)
            share_relay(late_keys, 1)

        @pl.when(tile == 1)
        def _():
            pass_on(first_part, 0)
            share_relay(late_values, 0)

        settle(tile, tiles)

        @pl.when(tile == 0)
        def _():
            pass_on(late_values, 2)
            share_relay(late_keys, 2)

    drain(final_keys)
    query_copy(final - 1).wait()
    gather(late_keys)
    pass_on(first_part, 1)
    share_relay(late_values, 1)

    @pl.loop(0, tiles)
    def _(tile):
        score(final - 1, tile, tile)

        @pl.when(tile == 0)
        def _():
            share_relay(late_values, 2)
            pass_on(last_part, 0)

    share_relay(first_part, 0)
    gather(late_values)

    @pl.loop(0, tiles)
    def _(tile):
        mix(final - 1, tile)

        @pl.when(tile == 0)
        def _():
            share_relay(first_part, 1)

        @pl.when(tile == 1)
        def _():
            share_relay(last_part, 0)

    drain(late_keys)
    drain(late_values)
    gather(first_part)

    @pl.loop(0, tiles)
    def _(tile):
        sums[tile] = collect(0, tile)

    gather(last_part)

    @pl.loop(0, tiles)
    def _(tile):
        summed = sums[tile] + collect(1, tile)
        out[tile, :, strip(final)] = (summed / totals[tile]).astype(out.dtype)

    drain(first_part)
    drain(last_part)


def on_device(count, queries, keys, values, neighbours):
    tokens, width = queries.shape
    tiles, slots = neighbours.shape
    tile_len = tokens // tiles
    heads = width // HD
    shape = (tiles, tile_len, width)
    lengths = [tile_len] * (2 * heads - 1) + [tile_len - ROWS, ROWS]
    windows = [pltpu.VMEM((WINDOW * tiles, length, HD), queries.dtype) for length in lengths]
    column = pltpu.VMEM((tiles, tile_len, HD), jnp.float32)
    pieces = tile_len // ROWS
    sends = pltpu.SemaphoreType.DMA((SENDS,))
    relays = pltpu.SemaphoreType.DMA((RELAYS,))
    hbm = pl.BlockSpec(memory_space=pl.ANY)
    neighbours = pltpu.with_memory_space_constraint(neighbours, pltpu.HBM)
    out = pl.pallas_call(
        functools.partial(kernel, count, heads),
        out_shape=jax.ShapeDtypeStruct(shape, queries.dtype),
        in_specs=[hbm, hbm, hbm, hbm],
        out_specs=pl.BlockSpec(memory_space=pltpu.VMEM),
        scratch_shapes=windows
        + [
            pltpu.VMEM((tiles + 1, slots, tile_len, tile_len), jnp.float32),
            pltpu.VMEM((tiles + 1, tile_len, HD), jnp.float32),
            pltpu.VMEM((tiles, tile_len, slots * lengths[-2]), jnp.bfloat16),
            pltpu.VMEM((tiles, tile_len, slots * lengths[-1]), jnp.bfloat16),
            pltpu.VMEM((slots * lengths[-2], HD), queries.dtype),
            pltpu.VMEM((slots * lengths[-1], HD), queries.dtype),
            column,
            column,
            pltpu.VMEM(shape, queries.dtype),
            pltpu.SMEM((tiles, slots), jnp.int32),
            pltpu.SemaphoreType.DMA,
            sends,
            pltpu.SemaphoreType.DMA((QUERIES,)),
        ]
        + [sends, pltpu.SemaphoreType.DMA((SENDS, pieces)), sends, pltpu.SemaphoreType.DMA((LANDS,))]
        + [relays, pltpu.SemaphoreType.DMA((LANDS, pieces)), relays, pltpu.SemaphoreType.DMA((SHARES + 1,))]
        + [pltpu.SemaphoreType.DMA, pltpu.SemaphoreType.REGULAR],
        compiler_params=pltpu.CompilerParams(
            collective_id=0, has_side_effects=True, vmem_limit_bytes=51 * 1024 * 1024
        ),
    )(neighbours, queries.reshape(shape), keys.reshape(shape), values.reshape(shape))
    return out.reshape(tokens, width)


def solution(mesh):
    spec = P(("groups", "blk"), None)
    return jax.shard_map(
        functools.partial(on_device, mesh.shape["blk"]),
        mesh=mesh, in_specs=(spec,) * 4, out_specs=spec, check_vma=False,
    )
```
